32 devices in a mesh: dp: 4 (over z), tensor: 8 (over y, x, core).
Axes of the slice: x: 2, y: 2, z: 4, core: 2. Of those that a mesh axis runs over, the one named last changes fastest.
Arguments:
- activations: bfloat16 [3072, 4096], P('dp', 'tensor'), may hold values from -6 to 6
- out_grads_t: bfloat16 [5504, 3072], P('tensor', 'dp'), may hold values from -6 to 6
- in_basis: bfloat16 [4096, 4096], P(None, 'tensor'), may hold values from -0.09375 to 0.09375
- out_basis_t: bfloat16 [5504, 5504], P('tensor'), may hold values from -0.078125 to 0.078125
- query_proj: bfloat16 [4, 5504, 4096], P(None, 'tensor', 'dp'), may hold values from -6 to 6
- eigvals: float32 [5504, 4096], P('tensor', 'dp'), may hold values from 0.05 to 5
- damping: float32 [1], replicated, may hold values from 0.05 to 0.2
- lengths: int32 [24], P('dp'), may hold values from 1 to 128, 1920 in all
Outputs:
- scores: float32 [24, 4], P('dp')
The draws below stay inside these ranges and needn't reach their ends.
Inputs may be any that keep to these rules, and one draw needn't show every extreme that they name: `lengths`: the largest token count is exactly 128.
All inputs are finite; a program needn't handle non-finite values. No bound on the sum of `lengths` on one device may be relied on, other than what follows from the above.
Results may differ from the reference program's by a relative error of at most 0.006.
Values may be sent and summed in bfloat16 or wider, within the bound.
A program may use at most 128 MiB of HBM per device.

```python
import math
import jax
import jax.numpy as jnp
import numpy as np
from jax import lax

D = 4096
FF = 5504
QUERIES = 4
SEQ_LEN = 128
SEQS = 24
TOKENS = 3072


def steps_of(rng, shape, shards, least, top_value):
    def one(dim, parts):
        heights = jax.random.uniform(jax.random.fold_in(jax.random.fold_in(rng, 6), dim), (parts,), jnp.float32, least / len(shards), top_value / len(shards))
        return jnp.repeat(jnp.exp(heights), shape[dim] // parts).reshape((-1,) + (1,) * (len(shape) - dim - 1))

    factor_of = one(*shards[0])
    for cut in shards[1:]:
        factor_of = factor_of * one(*cut)
    return factor_of


def split_up(count, total, limit, lean):
    loads = [(1 << 20) // math.isqrt(standing ** lean) + 1 for standing in range(2, count + 1)]
    spare, counts = total - limit - (count - 1), [1] * (count - 1)
    while spare > 0:
        candidates = [i for i in range(count - 1) if counts[i] < limit]
        mass, budget = sum([loads[i] for i in candidates]), spare
        for i in candidates:
            more = min(limit - counts[i], max(1, budget * loads[i] // mass), spare)
            counts[i] = counts[i] + more
            spare = spare - more
    return np.array([limit] + counts)


def ragged_sizes(rng, count, total, limit, slope):
    if count == 2:
        one = jax.random.randint(rng, (), max(1, total - limit), min(limit, total - 1) + 1)
        return jnp.stack([one, total - one])
    sizes = jnp.asarray(split_up(count, total, limit, slope), jnp.int32)
    twos = (count - 1) // 2
    donor, taker = sizes[1:1 + 2 * twos:2], sizes[2:2 + 2 * twos:2]
    slack = jnp.minimum(donor - 1, limit - taker)
    passed = jax.random.randint(jax.random.fold_in(rng, 1), (twos,), 0, 1 << 20) % (slack + 1)
    sizes = sizes.at[1:1 + 2 * twos:2].set(donor - passed).at[2:2 + 2 * twos:2].set(taker + passed)
    return sizes[jax.random.permutation(jax.random.fold_in(rng, 2), count)]


def gaussian(own_key, dims, deviation, bound, shards=(), kind=jnp.bfloat16):
    values = deviation * jax.random.normal(own_key, dims, jnp.float32)
    if shards:
        values = values * steps_of(own_key, dims, shards, -0.22, 0.18)
    return jnp.clip(values, -bound, bound).astype(kind)


def setup_inputs(seed: int = 0) -> dict:
    streams_of = jax.random.split(jax.random.key(seed), 9)
    return {
        "activations": gaussian(streams_of[0], (TOKENS, D), 1.0, 6.0, ((0, 4), (1, 8))),
        "out_grads_t": gaussian(streams_of[1], (FF, TOKENS), 1.0, 6.0, ((0, 8), (1, 4))),
        "in_basis": gaussian(streams_of[2], (D, D), D ** -0.5, 0.09375, ((1, 8),)),
        "out_basis_t": gaussian(streams_of[3], (FF, FF), FF ** -0.5, 0.078125, ((0, 8),)),
        "query_proj": gaussian(streams_of[4], (QUERIES, FF, D), 1.0, 6.0, ((1, 8), (2, 4))),
        "eigvals": jnp.clip(jnp.exp(math.log(5.0) - 4.6051702 * jax.random.uniform(streams_of[5], (FF, D), jnp.float32) ** steps_of(streams_of[5], (FF, D), ((0, 8), (1, 4)), -0.2, 0.2)), 0.05, 5.0),
        "damping": jnp.clip(jax.random.uniform(streams_of[6], (1,), jnp.float32, 0.05, 0.2), 0.05, 0.2),
        "lengths": ragged_sizes(streams_of[7], SEQS, SEQS * SEQ_LEN * 5 // 8, SEQ_LEN, 1).astype(jnp.int32),
    }


def reference(activations, out_grads_t, in_basis, out_basis_t, query_proj, eigvals, damping, lengths):
    act_proj = jnp.dot(activations, in_basis, preferred_element_type=jnp.float32).astype(jnp.bfloat16)
    grad_full = jnp.dot(out_basis_t, out_grads_t, preferred_element_type=jnp.float32)
    position = lax.broadcasted_iota(jnp.int32, (SEQS, SEQ_LEN), 1)
    keep = (position < lengths[:, None]).astype(jnp.float32).reshape(1, SEQS * SEQ_LEN)
    grad_proj = (grad_full * keep).astype(jnp.bfloat16)
    scaled = (query_proj.astype(jnp.float32) / (eigvals + damping[0])).astype(jnp.bfloat16)
    scaled_wide = scaled.astype(jnp.float32)

    def one_sequence(index):
        start = (index * SEQ_LEN).astype(jnp.int32)
        grad_cols = lax.dynamic_slice_in_dim(grad_proj, start, SEQ_LEN, 1)
        act_rows = lax.dynamic_slice_in_dim(act_proj, start, SEQ_LEN, 0)
        projected = jnp.dot(grad_cols, act_rows, preferred_element_type=jnp.float32)
        return jnp.einsum("ij,qij->q", projected, scaled_wide)

    totals = lax.map(one_sequence, jnp.arange(SEQS, dtype=jnp.int32))
    return totals * ((D * FF * SEQ_LEN) ** -0.5)
```

```python
import jax
import jax.numpy as jnp
from jax import lax
from jax.sharding import PartitionSpec as P


def local(activations, out_grads_t, in_basis, out_basis_t, query_proj, eigvals, damping, lengths):
    bf16, f32 = jnp.bfloat16, jnp.float32
    seq_count = lengths.shape[0]
    full_act = lax.all_gather(activations, "tensor", axis=1, tiled=True)
    token_rows = full_act.shape[0]
    seq_len = token_rows // seq_count
    act_local = jnp.dot(full_act, in_basis, preferred_element_type=f32).astype(bf16)
    act_full = lax.all_gather(act_local, "tensor", axis=1, tiled=True)
    features = act_full.shape[1]
    act_proj = lax.all_to_all(act_full, "dp", split_axis=1, concat_axis=0, tiled=True)
    grad_full = jnp.dot(
        out_basis_t, lax.all_gather(out_grads_t, "tensor", axis=0, tiled=True), preferred_element_type=f32
    )
    position = lax.broadcasted_iota(jnp.int32, (seq_count, seq_len), 1)
    keep = (position < lengths[:, None]).astype(f32).reshape(1, token_rows)
    grad_local = (grad_full * keep).astype(bf16)
    grad_proj = lax.all_gather(grad_local, "dp", axis=1, tiled=True)
    scaled = (query_proj.astype(f32) / (eigvals + damping[0])).astype(bf16)
    mixed = jnp.einsum("td,qjd->qjt", act_proj, scaled, preferred_element_type=f32)
    weighted = mixed * grad_proj.astype(f32)[None, :, :]
    query_count, width, tokens = weighted.shape
    partial_value = jnp.sum(weighted.reshape(query_count, width, tokens // seq_len, seq_len), axis=(1, 3)).T
    totals = lax.psum(partial_value, ("dp", "tensor"))
    mine = lax.dynamic_slice_in_dim(totals, lax.axis_index("dp") * seq_count, seq_count, 0)
    norm_factor = (features * out_basis_t.shape[1] * seq_len) ** (-0.5)
    return mine * norm_factor


def solution(mesh):
    placed = (
        P("dp", "tensor"),
        P("tensor", "dp"),
        P(None, "tensor"),
        P("tensor", None),
        P(None, "tensor", "dp"),
        P("tensor", "dp"),
        P(),
        P("dp"),
    )
    return jax.shard_map(
        local, mesh=mesh, in_specs=placed, out_specs=P("dp", None), check_vma=False
    )
```

```python
import functools

import jax
import jax.numpy as jnp
from jax import lax
from jax.experimental import pallas as pl
from jax.experimental.pallas import tpu as pltpu
from jax.sharding import PartitionSpec as P


def generic(activations, out_grads_t, in_basis, out_basis_t, query_proj, eigvals, damping, lengths):
    bf16, f32 = jnp.bfloat16, jnp.float32
    seq_count = lengths.shape[0]
    full_act = lax.all_gather(activations, "tensor", axis=1, tiled=True)
    token_rows = full_act.shape[0]
    seq_len = token_rows // seq_count
    act_local = jnp.dot(full_act, in_basis, preferred_element_type=f32).astype(bf16)
    act_full = lax.all_gather(act_local, "tensor", axis=1, tiled=True)
    features = act_full.shape[1]
    act_proj = lax.all_to_all(act_full, "dp", split_axis=1, concat_axis=0, tiled=True)
    grad_full = jnp.dot(
        out_basis_t, lax.all_gather(out_grads_t, "tensor", axis=0, tiled=True), preferred_element_type=f32
    )
    position = lax.broadcasted_iota(jnp.int32, (seq_count, seq_len), 1)
    keep = (position < lengths[:, None]).astype(f32).reshape(1, token_rows)
    grad_local = (grad_full * keep).astype(bf16)
    grad_proj = lax.all_gather(grad_local, "dp", axis=1, tiled=True)
    scaled = (query_proj.astype(f32) / (eigvals + damping[0])).astype(bf16)
    mixed = jnp.einsum("td,qjd->qjt", act_proj, scaled, preferred_element_type=f32)
    weighted = mixed * grad_proj.astype(f32)[None, :, :]
    query_count, width, tokens = weighted.shape
    partial_value = jnp.sum(weighted.reshape(query_count, width, tokens // seq_len, seq_len), axis=(1, 3)).T
    totals = lax.psum(partial_value, ("dp", "tensor"))
    mine = lax.dynamic_slice_in_dim(totals, lax.axis_index("dp") * seq_count, seq_count, 0)
    norm_factor = (features * out_basis_t.shape[1] * seq_len) ** (-0.5)
    return mine * norm_factor


MESH = pl.DeviceIdType.MESH
CHUNK = 256


def kernel(
    planes, seq_len, act_ref, og_ref, in_ref, out_ref, query_ref, eig_ref, keep_ref, damp_ref, res_ref,
    og_all, act_all, in_b, out_b, scaled, eig, a_all, a_part, a_loc, a_acc, g_all, g_acc, csum, tiles, got_z, got_p,
    load_sem, gs_send, gs_recv, up_send, up_recv, dn_send, dn_recv, xp_send, xp_recv, xz_send, xz_recv,
    rz_send, rz_recv, rp_send, rp_recv,
):
    bf16, f32 = jnp.bfloat16, jnp.float32
    z, j = lax.axis_index("dp"), lax.axis_index("tensor")
    members = act_all.shape[0]
    rows, feats = act_ref.shape
    width, tokens = og_ref.shape
    depth = out_b.shape[1]
    queries, span = scaled.shape[0], scaled.shape[2]
    part = rows // members
    chunks = tokens // CHUNK
    jx = j + 2 - 4 * lax.rem(j // 2, 2)
    jy = j + 4 - 8 * (j // 4)
    jd = jx + 4 - 8 * (j // 4)

    def mate(k):
        return k + 1 - 2 * lax.rem(k, 2)

    jp = mate(j)

    loads = [
        pltpu.make_async_copy(og_ref, og_all.at[pl.ds(pl.multiple_of(j * width, 16), width), :], load_sem.at[0]),
        pltpu.make_async_copy(act_ref, act_all.at[j], load_sem.at[1]),
        pltpu.make_async_copy(query_ref, scaled, load_sem.at[2]),
        pltpu.make_async_copy(eig_ref, eig, load_sem.at[3]),
        pltpu.make_async_copy(out_ref, out_b, load_sem.at[4]),
        pltpu.make_async_copy(in_ref, in_b, load_sem.at[5]),
    ]
    for load in loads:
        load.start()

    barrier = pltpu.get_barrier_semaphore()
    for step in range(1, members):
        pl.semaphore_signal(barrier, inc=1, device_id={"tensor": lax.rem(j + step, members)}, device_id_type=MESH)
    for step in range(1, planes):
        pl.semaphore_signal(barrier, inc=1, device_id={"dp": lax.rem(z + step, planes)}, device_id_type=MESH)
    pl.semaphore_wait(barrier, members + planes - 2)

    def og_view(k, h):
        if h is None:
            return og_all.at[pl.ds(pl.multiple_of(k * width, 16), width), :]
        return og_all.at[pl.ds(pl.multiple_of(k * width, 16), width), pl.ds(h * (tokens // 2), tokens // 2)]

    def act_view(k, h):
        if h is None:
            return act_all.at[k]
        return act_all.at[k, pl.ds(h * (rows // 2), rows // 2), :]

    def a_view(k, h):
        at = pl.ds(pl.multiple_of(k * part, 16), part)
        if h is None:
            return a_all.at[:, at, :]
        return a_all.at[pl.ds(h * (planes // 2), planes // 2), at, :]

    class Gather:
        def __init__(self, op, view, own):
            self.op, self.view, self.own = op, view, own
            self.plan = [
                (j, 0, jx), (j, 1, jx), (jy, 1, jx),
                (j, 1, jy), (j, 0, jy), (jx, 0, jy),
                (j, None, jp), (jx, None, jp), (jy, None, jp), (jd, 0, jp), (jd, 1, jp),
            ]
            self.landed = [
                (jx, 0), (jx, 1), (jd, 1),
                (jy, 1), (jy, 0), (jd, 0),
                (jp, None), (mate(jx), None), (mate(jy), None), (mate(jd), 0), (mate(jd), 1),
            ]

        def copy(self, slot):
            block, half, target = self.plan[slot]
            src = self.own(half) if slot in (0, 1, 3, 4, 6) else self.view(block, half)
            return pltpu.make_async_remote_copy(
                src_ref=src, dst_ref=self.view(block, half), send_sem=gs_send.at[self.op, slot],
                recv_sem=gs_recv.at[self.op, slot], device_id={"tensor": target}, device_id_type=MESH,
            )

        def start(self, *slots):
            for slot in slots:
                self.copy(slot).start()

        def arrive(self, *slots):
            for slot in slots:
                block, half = self.landed[slot]
                view = self.view(block, half)
                pltpu.make_async_remote_copy(
                    src_ref=view, dst_ref=view, send_sem=gs_send.at[self.op, slot],
                    recv_sem=gs_recv.at[self.op, slot], device_id={"tensor": jp}, device_id_type=MESH,
                ).wait_recv()

        def begin(self):
            self.start(0, 3, 1, 4, 6)

        def relay(self):
            self.arrive(0)
            self.start(5)
            self.arrive(3)
            self.start(2)

        def share_near(self):
            self.arrive(1)
            self.start(7)
            self.arrive(4)
            self.start(8)

        def share_far(self):
            self.arrive(5)
            self.start(9)
            self.arrive(2)
            self.start(10)

        def drain(self):
            for slot in range(len(self.plan)):
                self.copy(slot).wait_send()

    def half_of(ref, h, axis):
        if h is None:
            return ref
        size = ref.shape[axis] // 2
        return ref.at[pl.ds(h * size, size), :] if axis == 0 else ref.at[:, pl.ds(h * size, size)]

    og = Gather(0, og_view, lambda h: half_of(og_ref, h, 1))
    act = Gather(1, act_view, lambda h: half_of(act_ref, h, 0))
    acts = Gather(2, a_view, lambda h: a_view(j, h))

    og.begin()
    csum[...] = jnp.zeros_like(csum)

    loads[2].wait()
    loads[3].wait()
    step_rows = 16

    def scale(i, carry):
        at = pl.ds(pl.multiple_of(i * step_rows, step_rows), step_rows)
        below = eig[at, :] + damp_ref[0]
        for q in range(queries):
            scaled[q, at, :] = (scaled[q, at, :].astype(f32) / below).astype(bf16)
        return carry

    lax.fori_loop(0, width // step_rows, scale, 0)

    og.relay()
    act.begin()
    og.share_near()
    og.share_far()
    og.arrive(6, 7, 8, 9, 10)
    loads[0].wait()
    loads[4].wait()

    def up(block, n):
        return pltpu.make_async_remote_copy(
            src_ref=g_all.at[block, n], dst_ref=g_all.at[block, n], send_sem=up_send.at[block, n],
            recv_sem=up_recv.at[block, n], device_id={"dp": lax.rem(z + 1, planes)}, device_id_type=MESH,
        )

    def down(block, n):
        return pltpu.make_async_remote_copy(
            src_ref=g_all.at[block, n], dst_ref=g_all.at[block, n], send_sem=dn_send.at[block, n],
            recv_sem=dn_recv.at[block, n], device_id={"dp": lax.rem(z + planes - 1, planes)}, device_id_type=MESH,
        )

    top, bottom = z == planes - 1, z == 0

    def service(level, n):
        @pl.when(z - level >= 0)
        def _():
            up(z - level, n).wait_recv()

        @pl.when((z - level >= 0) & (z < planes - 1))
        def _():
            up(z - level, n).start()

        @pl.when(z + level < planes)
        def _():
            down(z + level, n).wait_recv()

        @pl.when((z + level < planes) & (z > 0))
        def _():
            down(z + level, n).start()

    k_tile = 3 * CHUNK
    k_full = depth // k_tile

    def project(n, carry):
        at = pl.ds(pl.multiple_of(n * CHUNK, CHUNK), CHUNK)
        k_rest = depth - k_full * k_tile
        if k_rest:
            g_acc[...] = jnp.dot(
                out_b[:, pl.ds(k_full * k_tile, k_rest)], og_all[pl.ds(k_full * k_tile, k_rest), at],
                preferred_element_type=f32,
            )
        else:
            g_acc[...] = jnp.zeros_like(g_acc)

        def inner(k, c):
            deep = pl.ds(pl.multiple_of(k * k_tile, k_tile), k_tile)
            g_acc[...] += jnp.dot(out_b[:, deep], og_all[deep, at], preferred_element_type=f32)
            return c

        lax.fori_loop(0, k_full, inner, 0)
        g_all[z, n] = (g_acc[...] * keep_ref[0:1, at]).astype(bf16)

        @pl.when(z < planes - 1)
        def _():
            up(z, n).start()

        @pl.when(z > 0)
        def _():
            down(z, n).start()

        return carry

    lax.fori_loop(0, chunks, project, 0)

    a_acc[...] = jnp.zeros_like(a_acc)
    loads[1].wait()
    loads[5].wait()

    def contract(first):
        def body(i, carry):
            k = first + i * (mate(first) - first)
            deep = pl.ds(pl.multiple_of(k * feats, feats), feats)
            a_acc[...] += jnp.dot(act_all[k], in_b[deep, :], preferred_element_type=f32)
            return carry

        lax.fori_loop(0, 2, body, 0)

    act.relay()
    act.arrive(6)
    contract(j)
    act.share_near()
    service(1, 0)
    act.arrive(7)
    contract(jx)
    act.arrive(8)
    contract(jy)
    act.share_far()
    act.arrive(9, 10)
    contract(jd)
    a_loc[...] = a_acc[...].astype(bf16)

    def spread(to):
        return pltpu.make_async_remote_copy(
            src_ref=a_loc.at[pl.ds(pl.multiple_of(to * part, 16), part), :],
            dst_ref=a_part.at[j], send_sem=xp_send.at[to], recv_sem=xp_recv.at[j],
            device_id={"tensor": to}, device_id_type=MESH,
        )

    def spread_from(k):
        return pltpu.make_async_remote_copy(
            src_ref=a_part.at[k], dst_ref=a_part.at[k], send_sem=xp_send.at[k], recv_sem=xp_recv.at[k],
            device_id={"tensor": k}, device_id_type=MESH,
        )

    for step in range(1, members):
        spread(lax.rem(j + step, members)).start()
    a_part[j] = a_loc[pl.ds(pl.multiple_of(j * part, 16), part), :]
    service(1, 1)
    for step in range(1, members):
        spread_from(lax.rem(j + step, members)).wait_recv()

    mine = pl.ds(pl.multiple_of(j * part, 16), part)
    group = span // a_part.shape[2]

    def lift(to, g):
        lane = pl.ds(g * a_part.shape[2], a_part.shape[2])
        return pltpu.make_async_remote_copy(
            src_ref=a_part.at[to * group + g], dst_ref=a_all.at[z, mine, lane], send_sem=xz_send.at[to, g],
            recv_sem=xz_recv.at[z, g], device_id={"dp": to}, device_id_type=MESH,
        )

    def lift_from(k, g):
        lane = pl.ds(g * a_part.shape[2], a_part.shape[2])
        view = a_all.at[k, mine, lane]
        return pltpu.make_async_remote_copy(
            src_ref=view, dst_ref=view, send_sem=xz_send.at[k, g], recv_sem=xz_recv.at[k, g],
            device_id={"dp": k}, device_id_type=MESH,
        )

    for step in range(1, planes):
        for g in range(group):
            lift(lax.rem(z + step, planes), g).start()
    for g in range(group):
        a_all[z, mine, pl.ds(g * a_part.shape[2], a_part.shape[2])] = a_part[z * group + g]
    for n in range(2, chunks):
        service(1, n)
    for step in range(1, planes):
        for g in range(group):
            lift_from(lax.rem(z + step, planes), g).wait_recv()

    acts.begin()
    service(2, 0)
    acts.relay()
    acts.share_near()
    for n in range(1, chunks):
        service(2, n)
    acts.share_far()
    acts.arrive(6, 7, 8, 9, 10)

    turn = 1 - 2 * (z // (planes // 2))
    for s in range(planes):
        block = lax.rem(z + s * turn + planes, planes)

        def score(n, carry, s=s, block=block):
            if s > 2:
                service(s, n)
            at = pl.ds(pl.multiple_of(n * CHUNK, CHUNK), CHUNK)
            for q in range(queries):
                mixed = lax.dot_general(
                    scaled[q], a_all[block, at, :], (((1,), (1,)), ((), ())), preferred_element_type=f32
                )
                csum[block, n, pl.ds(q, 1), :] = jnp.sum(
                    mixed * g_all[block, n].astype(f32), axis=0, keepdims=True
                )
            return carry

        lax.fori_loop(0, chunks, score, 0)

    per = res_ref.shape[1]
    lane_at = lax.broadcasted_iota(jnp.int32, (8, per), 1)
    each = CHUNK // seq_len
    for b in range(planes):
        tile = jnp.zeros((8, per), f32)
        for n in range(chunks):
            for h in range(each):
                total = jnp.sum(csum[b, n, :, h * seq_len:(h + 1) * seq_len], axis=1, keepdims=True)
                tile = tile + jnp.where(lane_at == n * each + h, total, 0.0)
        tiles[b] = tile

    def fold(to):
        return pltpu.make_async_remote_copy(
            src_ref=tiles.at[to], dst_ref=got_z.at[z], send_sem=rz_send.at[to], recv_sem=rz_recv.at[z],
            device_id={"dp": to}, device_id_type=MESH,
        )

    def fold_from(k):
        return pltpu.make_async_remote_copy(
            src_ref=got_z.at[k], dst_ref=got_z.at[k], send_sem=rz_send.at[k], recv_sem=rz_recv.at[k],
            device_id={"dp": k}, device_id_type=MESH,
        )

    for step in range(1, planes):
        fold(lax.rem(z + step, planes)).start()
    got_z[z] = tiles[z]
    for step in range(1, planes):
        fold_from(lax.rem(z + step, planes)).wait_recv()
    total = got_z[0]
    for b in range(1, planes):
        total = total + got_z[b]
    got_p[j] = total

    def share(to):
        return pltpu.make_async_remote_copy(
            src_ref=got_p.at[j], dst_ref=got_p.at[j], send_sem=rp_send.at[to], recv_sem=rp_recv.at[j],
            device_id={"tensor": to}, device_id_type=MESH,
        )

    def share_from(k):
        return pltpu.make_async_remote_copy(
            src_ref=got_p.at[k], dst_ref=got_p.at[k], send_sem=rp_send.at[k], recv_sem=rp_recv.at[k],
            device_id={"tensor": k}, device_id_type=MESH,
        )

    for step in range(1, members):
        share(lax.rem(j + step, members)).start()
    for step in range(1, members):
        share_from(lax.rem(j + step, members)).wait_recv()
    total = got_p[0]
    for k in range(1, members):
        total = total + got_p[k]
    res_ref[...] = total

    og.drain()
    act.drain()
    acts.drain()
    for level in range(planes):
        for n in range(chunks):
            @pl.when((z - level >= 0) & (z < planes - 1))
            def _():
                up(z - level, n).wait_send()

            @pl.when((z + level < planes) & (z > 0))
            def _():
                down(z + level, n).wait_send()
    for step in range(1, members):
        to = lax.rem(j + step, members)
        spread(to).wait_send()
        share(to).wait_send()
    for step in range(1, planes):
        to = lax.rem(z + step, planes)
        for g in range(group):
            lift(to, g).wait_send()
        fold(to).wait_send()


def fits(planes, members, activations, out_grads_t, in_basis, query_proj, seq_count):
    rows, feats = activations.shape
    width, tokens = out_grads_t.shape
    cols, span = in_basis.shape[1], query_proj.shape[2]
    return (
        members == 8 and planes % 2 == 0 and rows == tokens and rows % (16 * members) == 0
        and feats % 128 == 0 and cols % 128 == 0 and span % cols == 0 and width % 16 == 0
        and tokens % CHUNK == 0 and CHUNK % (rows // seq_count) == 0 and (rows // seq_count) % 128 == 0
        and seq_count <= 128 and query_proj.shape[0] <= 8
    )


def local(planes, members, activations, out_grads_t, in_basis, out_basis_t, query_proj, eigvals, damping, lengths):
    seq_count = lengths.shape[0]
    if not fits(planes, members, activations, out_grads_t, in_basis, query_proj, seq_count):
        return generic(activations, out_grads_t, in_basis, out_basis_t, query_proj, eigvals, damping, lengths)
    bf16, f32 = jnp.bfloat16, jnp.float32
    rows, feats = activations.shape
    width, tokens = out_grads_t.shape
    features, cols = in_basis.shape
    depth = out_basis_t.shape[1]
    queries, _, span = query_proj.shape
    seq_len = rows // seq_count
    part, chunks, group = rows // members, tokens // CHUNK, span // cols
    position = lax.broadcasted_iota(jnp.int32, (seq_count, seq_len), 1)
    keep = jnp.broadcast_to((position < lengths[:, None]).astype(f32).reshape(1, tokens), (8, tokens))
    any_space = pl.BlockSpec(memory_space=pl.ANY)
    vmem = pl.BlockSpec(memory_space=pltpu.VMEM)
    dma = pltpu.SemaphoreType.DMA
    res = pl.pallas_call(
        functools.partial(kernel, planes, seq_len),
        out_shape=jax.ShapeDtypeStruct((8, 128), f32),
        in_specs=[any_space] * 6 + [vmem, pl.BlockSpec(memory_space=pltpu.SMEM)],
        out_specs=vmem,
        scratch_shapes=[
            pltpu.VMEM((members * width, tokens), bf16),
            pltpu.VMEM((members, rows, feats), bf16),
            pltpu.VMEM((features, cols), bf16),
            pltpu.VMEM((width, depth), bf16),
            pltpu.VMEM((queries, width, span), bf16),
            pltpu.VMEM((width, span), f32),
            pltpu.VMEM((planes, rows, span), bf16),
            pltpu.VMEM((members, part, cols), bf16),
            pltpu.VMEM((rows, cols), bf16),
            pltpu.VMEM((rows, cols), f32),
            pltpu.VMEM((planes, chunks, width, CHUNK), bf16),
            pltpu.VMEM((width, CHUNK), f32),
            pltpu.VMEM((planes, chunks, 8, CHUNK), f32),
            pltpu.VMEM((planes, 8, 128), f32),
            pltpu.VMEM((planes, 8, 128), f32),
            pltpu.VMEM((members, 8, 128), f32),
            dma((6,)), dma((3, 11)), dma((3, 11)),
            dma((planes, chunks)), dma((planes, chunks)), dma((planes, chunks)), dma((planes, chunks)),
            dma((members,)), dma((members,)), dma((planes, group)), dma((planes, group)),
            dma((planes,)), dma((planes,)), dma((members,)), dma((members,)),
        ],
        compiler_params=pltpu.CompilerParams(
            collective_id=0, has_side_effects=True, vmem_limit_bytes=63 * 1024 * 1024
        ),
    )(activations, out_grads_t, in_basis, out_basis_t, query_proj, eigvals, keep, damping)
    norm_factor = (features * depth * seq_len) ** (-0.5)
    return res[:queries, :seq_count].T * norm_factor


def solution(mesh):
    placed = (
        P("dp", "tensor"),
        P("tensor", "dp"),
        P(None, "tensor"),
        P("tensor", None),
        P(None, "tensor", "dp"),
        P("tensor", "dp"),
        P(),
        P("dp"),
    )
    return jax.shard_map(
        functools.partial(local, mesh.shape["dp"], mesh.shape["tensor"]), mesh=mesh, in_specs=placed, out_specs=P("dp", None), check_vma=False
    )
```

```python
import functools

import jax
import jax.numpy as jnp
from jax import lax
from jax.experimental import pallas as pl
from jax.experimental.pallas import tpu as pltpu
from jax.sharding import PartitionSpec as P


def generic(activations, out_grads_t, in_basis, out_basis_t, query_proj, eigvals, damping, lengths):
    bf16, f32 = jnp.bfloat16, jnp.float32
    seq_count = lengths.shape[0]
    full_act = lax.all_gather(activations, "tensor", axis=1, tiled=True)
    token_rows = full_act.shape[0]
    seq_len = token_rows // seq_count
    act_local = jnp.dot(full_act, in_basis, preferred_element_type=f32).astype(bf16)
    act_full = lax.all_gather(act_local, "tensor", axis=1, tiled=True)
    features = act_full.shape[1]
    act_proj = lax.all_to_all(act_full, "dp", split_axis=1, concat_axis=0, tiled=True)
    grad_full = jnp.dot(
        out_basis_t, lax.all_gather(out_grads_t, "tensor", axis=0, tiled=True), preferred_element_type=f32
    )
    position = lax.broadcasted_iota(jnp.int32, (seq_count, seq_len), 1)
    keep = (position < lengths[:, None]).astype(f32).reshape(1, token_rows)
    grad_local = (grad_full * keep).astype(bf16)
    grad_proj = lax.all_gather(grad_local, "dp", axis=1, tiled=True)
    scaled = (query_proj.astype(f32) / (eigvals + damping[0])).astype(bf16)
    mixed = jnp.einsum("td,qjd->qjt", act_proj, scaled, preferred_element_type=f32)
    weighted = mixed * grad_proj.astype(f32)[None, :, :]
    query_count, width, tokens = weighted.shape
    partial_value = jnp.sum(weighted.reshape(query_count, width, tokens // seq_len, seq_len), axis=(1, 3)).T
    totals = lax.psum(partial_value, ("dp", "tensor"))
    mine = lax.dynamic_slice_in_dim(totals, lax.axis_index("dp") * seq_count, seq_count, 0)
    norm_factor = (features * out_basis_t.shape[1] * seq_len) ** (-0.5)
    return mine * norm_factor


MESH = pl.DeviceIdType.MESH
CHUNK = 256


def kernel(
    planes, seq_len, act_ref, og_ref, in_ref, out_ref, query_ref, eig_ref, keep_ref, damp_ref, res_ref,
    og_all, act_all, in_b, out_b, scaled, eig, a_all, a_part, a_loc, a_acc, g_all, g_acc, csum, tiles, got_z, got_p,
    load_sem, gs_send, gs_recv, up_send, up_recv, dn_send, dn_recv, xp_send, xp_recv, xz_send, xz_recv,
    rz_send, rz_recv, rp_send, rp_recv,
):
    bf16, f32 = jnp.bfloat16, jnp.float32
    z, j = lax.axis_index("dp"), lax.axis_index("tensor")
    members = act_all.shape[0]
    rows, feats = act_ref.shape
    width, tokens = og_ref.shape
    depth = out_b.shape[1]
    queries, span = scaled.shape[0], scaled.shape[2]
    part = rows // members
    chunks = tokens // CHUNK
    jx = j + 2 - 4 * lax.rem(j // 2, 2)
    jy = j + 4 - 8 * (j // 4)
    jd = jx + 4 - 8 * (j // 4)

    def mate(k):
        return k + 1 - 2 * lax.rem(k, 2)

    jp = mate(j)

    loads = [
        pltpu.make_async_copy(og_ref, og_all.at[pl.ds(pl.multiple_of(j * width, 16), width), :], load_sem.at[0]),
        pltpu.make_async_copy(act_ref, act_all.at[j], load_sem.at[1]),
        pltpu.make_async_copy(query_ref, scaled, load_sem.at[2]),
        pltpu.make_async_copy(eig_ref, eig, load_sem.at[3]),
        pltpu.make_async_copy(out_ref, out_b, load_sem.at[4]),
        pltpu.make_async_copy(in_ref, in_b, load_sem.at[5]),
    ]
    for load in loads:
        load.start()

    barrier = pltpu.get_barrier_semaphore()
    for step in range(1, members):
        pl.semaphore_signal(barrier, inc=1, device_id={"tensor": lax.rem(j + step, members)}, device_id_type=MESH)
    for step in range(1, planes):
        pl.semaphore_signal(barrier, inc=1, device_id={"dp": lax.rem(z + step, planes)}, device_id_type=MESH)
    pl.semaphore_wait(barrier, members + planes - 2)

    cut = (width // 2 + 15) // 16 * 16

    def og_rows(h):
        return (0, width) if h is None else ((0, cut), (cut, width - cut))[h]

    def og_view(lanes):
        def view(k, h):
            first, size = og_rows(h)
            return og_all.at[pl.ds(pl.multiple_of(k * width + first, 16), size), lanes]

        return view

    def og_own(lanes):
        return lambda h: og_ref.at[pl.ds(*og_rows(h)), lanes]

    def act_view(k, h):
        if h is None:
            return act_all.at[k]
        return act_all.at[k, pl.ds(h * (rows // 2), rows // 2), :]

    def a_view(k, h):
        at = pl.ds(pl.multiple_of(k * part, 16), part)
        if h is None:
            return a_all.at[:, at, :]
        return a_all.at[pl.ds(h * (planes // 2), planes // 2), at, :]

    class Gather:
        def __init__(self, op, view, own):
            self.op, self.view, self.own = op, view, own
            self.plan = [
                (j, 0, jx), (j, 1, jx), (jy, 1, jx),
                (j, 1, jy), (j, 0, jy), (jx, 0, jy),
                (j, None, jp), (jx, None, jp), (jy, None, jp), (jd, 0, jp), (jd, 1, jp),
            ]
            self.landed = [
                (jx, 0), (jx, 1), (jd, 1),
                (jy, 1), (jy, 0), (jd, 0),
                (jp, None), (mate(jx), None), (mate(jy), None), (mate(jd), 0), (mate(jd), 1),
            ]

        def copy(self, slot):
            block, half, target = self.plan[slot]
            src = self.own(half) if slot in (0, 1, 3, 4, 6) else self.view(block, half)
            return pltpu.make_async_remote_copy(
                src_ref=src, dst_ref=self.view(block, half), send_sem=gs_send.at[self.op, slot],
                recv_sem=gs_recv.at[self.op, slot], device_id={"tensor": target}, device_id_type=MESH,
            )

        def start(self, *slots):
            for slot in slots:
                self.copy(slot).start()

        def arrive(self, *slots):
            for slot in slots:
                block, half = self.landed[slot]
                view = self.view(block, half)
                pltpu.make_async_remote_copy(
                    src_ref=view, dst_ref=view, send_sem=gs_send.at[self.op, slot],
                    recv_sem=gs_recv.at[self.op, slot], device_id={"tensor": jp}, device_id_type=MESH,
                ).wait_recv()

        def open(self):
            self.start(0, 3, 6)

        def extend(self):
            self.start(1, 4)

        def begin(self):
            self.start(0, 3, 1, 4, 6)

        def relay(self):
            self.arrive(0)
            self.start(5)
            self.arrive(3)
            self.start(2)

        def share_near(self):
            self.arrive(1)
            self.start(7)
            self.arrive(4)
            self.start(8)

        def share_far(self):
            self.arrive(5)
            self.start(9)
            self.arrive(2)
            self.start(10)

        def drain(self):
            for slot in range(len(self.plan)):
                self.copy(slot).wait_send()

    def act_own(h):
        return act_ref if h is None else act_ref.at[pl.ds(h * (rows // 2), rows // 2), :]

    early, late = pl.ds(0, CHUNK), pl.ds(CHUNK, tokens - CHUNK)
    og = Gather(0, og_view(early), og_own(early))
    act = Gather(1, act_view, act_own)
    more = Gather(3, og_view(late), og_own(late))
    acts = Gather(2, a_view, lambda h: a_view(j, h))

    og.begin()
    csum[...] = jnp.zeros_like(csum)

    loads[2].wait()
    loads[3].wait()
    step_rows = 16

    def scale(i, carry):
        at = pl.ds(pl.multiple_of(i * step_rows, step_rows), step_rows)
        below = eig[at, :] + damp_ref[0]
        for q in range(queries):
            scaled[q, at, :] = (scaled[q, at, :].astype(f32) / below).astype(bf16)
        return carry

    lax.fori_loop(0, width // step_rows, scale, 0)

    og.relay()
    act.begin()
    og.share_near()
    og.share_far()
    og.arrive(6, 7, 8, 9, 10)
    loads[0].wait()
    loads[4].wait()

    def up(block, n):
        return pltpu.make_async_remote_copy(
            src_ref=g_all.at[block, n], dst_ref=g_all.at[block, n], send_sem=up_send.at[block, n],
            recv_sem=up_recv.at[block, n], device_id={"dp": lax.rem(z + 1, planes)}, device_id_type=MESH,
        )

    def down(block, n):
        return pltpu.make_async_remote_copy(
            src_ref=g_all.at[block, n], dst_ref=g_all.at[block, n], send_sem=dn_send.at[block, n],
            recv_sem=dn_recv.at[block, n], device_id={"dp": lax.rem(z + planes - 1, planes)}, device_id_type=MESH,
        )

    top, bottom = z == planes - 1, z == 0

    def service(level, n):
        @pl.when(z - level >= 0)
        def _():
            up(z - level, n).wait_recv()

        @pl.when((z - level >= 0) & (z < planes - 1))
        def _():
            up(z - level, n).start()

        @pl.when(z + level < planes)
        def _():
            down(z + level, n).wait_recv()

        @pl.when((z + level < planes) & (z > 0))
        def _():
            down(z + level, n).start()

    k_tile = 3 * CHUNK
    k_full = depth // k_tile

    def project(n, carry):
        at = pl.ds(pl.multiple_of(n * CHUNK, CHUNK), CHUNK)
        k_rest = depth - k_full * k_tile
        if k_rest:
            g_acc[...] = jnp.dot(
                out_b[:, pl.ds(k_full * k_tile, k_rest)], og_all[pl.ds(k_full * k_tile, k_rest), at],
                preferred_element_type=f32,
            )
        else:
            g_acc[...] = jnp.zeros_like(g_acc)

        def inner(k, c):
            deep = pl.ds(pl.multiple_of(k * k_tile, k_tile), k_tile)
            g_acc[...] += jnp.dot(out_b[:, deep], og_all[deep, at], preferred_element_type=f32)
            return c

        lax.fori_loop(0, k_full, inner, 0)
        g_all[z, n] = (g_acc[...] * keep_ref[0:1, at]).astype(bf16)

        @pl.when(z < planes - 1)
        def _():
            up(z, n).start()

        @pl.when(z > 0)
        def _():
            down(z, n).start()

        return carry

    project(0, 0)

    a_acc[...] = jnp.zeros_like(a_acc)
    loads[1].wait()
    loads[5].wait()

    def contract(first):
        def body(i, carry):
            k = first + i * (mate(first) - first)
            deep = pl.ds(pl.multiple_of(k * feats, feats), feats)
            a_acc[...] += jnp.dot(act_all[k], in_b[deep, :], preferred_element_type=f32)
            return carry

        lax.fori_loop(0, 2, body, 0)

    act.relay()
    more.open()
    act.arrive(6)
    contract(j)
    act.share_near()
    service(1, 0)
    act.arrive(7)
    contract(jx)
    act.arrive(8)
    contract(jy)
    service(2, 0)
    act.share_far()
    act.arrive(9, 10)
    contract(jd)
    a_loc[...] = a_acc[...].astype(bf16)

    def spread(to):
        return pltpu.make_async_remote_copy(
            src_ref=a_loc.at[pl.ds(pl.multiple_of(to * part, 16), part), :],
            dst_ref=a_part.at[j], send_sem=xp_send.at[to], recv_sem=xp_recv.at[j],
            device_id={"tensor": to}, device_id_type=MESH,
        )

    def spread_from(k):
        return pltpu.make_async_remote_copy(
            src_ref=a_part.at[k], dst_ref=a_part.at[k], send_sem=xp_send.at[k], recv_sem=xp_recv.at[k],
            device_id={"tensor": k}, device_id_type=MESH,
        )

    for step in range(1, members):
        spread(lax.rem(j + step, members)).start()
    a_part[j] = a_loc[pl.ds(pl.multiple_of(j * part, 16), part), :]
    more.extend()
    more.relay()
    service(3, 0)
    for step in range(1, members):
        spread_from(lax.rem(j + step, members)).wait_recv()

    mine = pl.ds(pl.multiple_of(j * part, 16), part)
    group = span // a_part.shape[2]

    def lift(to, g):
        lane = pl.ds(g * a_part.shape[2], a_part.shape[2])
        return pltpu.make_async_remote_copy(
            src_ref=a_part.at[to * group + g], dst_ref=a_all.at[z, mine, lane], send_sem=xz_send.at[to, g],
            recv_sem=xz_recv.at[z, g], device_id={"dp": to}, device_id_type=MESH,
        )

    def lift_from(k, g):
        lane = pl.ds(g * a_part.shape[2], a_part.shape[2])
        view = a_all.at[k, mine, lane]
        return pltpu.make_async_remote_copy(
            src_ref=view, dst_ref=view, send_sem=xz_send.at[k, g], recv_sem=xz_recv.at[k, g],
            device_id={"dp": k}, device_id_type=MESH,
        )

    for step in range(1, planes):
        for g in range(group):
            lift(lax.rem(z + step, planes), g).start()
    for g in range(group):
        a_all[z, mine, pl.ds(g * a_part.shape[2], a_part.shape[2])] = a_part[z * group + g]
    more.share_near()
    more.share_far()
    for step in range(1, planes):
        for g in range(group):
            lift_from(lax.rem(z + step, planes), g).wait_recv()
    acts.begin()
    more.arrive(6, 7, 8, 9, 10)
    lax.fori_loop(1, chunks, project, 0)
    acts.relay()
    for n in range(1, chunks):
        service(1, n)
    acts.share_near()
    service(2, 1)
    acts.share_far()
    acts.arrive(6, 7, 8, 9, 10)
    for level in range(4, planes):
        service(level, 0)

    turn = 1 - 2 * (z // (planes // 2))

    def score(s, n):
        block = lax.rem(z + s * turn + planes, planes)
        at = pl.ds(pl.multiple_of(n * CHUNK, CHUNK), CHUNK)
        for q in range(queries):
            mixed = lax.dot_general(
                scaled[q], a_all[block, at, :], (((1,), (1,)), ((), ())), preferred_element_type=f32
            )
            csum[block, n, pl.ds(q, 1), :] = jnp.sum(mixed * g_all[block, n].astype(f32), axis=0, keepdims=True)

    def score_loop(lo, hi, n):
        def body(s, carry):
            score(s, n)
            return carry

        lax.fori_loop(lo, hi, body, 0)

    score_loop(0, planes, 0)
    for n in range(2, chunks):
        service(2, n)
    for n in range(1, chunks):
        score_loop(0, min(3, planes), n)
    for n in range(1, chunks):
        for level in range(3, planes):
            service(level, n)
        score_loop(min(3, planes), planes, n)

    per = res_ref.shape[1]
    lane_at = lax.broadcasted_iota(jnp.int32, (8, per), 1)
    each = CHUNK // seq_len
    for b in range(planes):
        tile = jnp.zeros((8, per), f32)
        for n in range(chunks):
            for h in range(each):
                total = jnp.sum(csum[b, n, :, h * seq_len:(h + 1) * seq_len], axis=1, keepdims=True)
                tile = tile + jnp.where(lane_at == n * each + h, total, 0.0)
        tiles[b] = tile

    def fold(to):
        return pltpu.make_async_remote_copy(
            src_ref=tiles.at[to], dst_ref=got_z.at[z], send_sem=rz_send.at[to], recv_sem=rz_recv.at[z],
            device_id={"dp": to}, device_id_type=MESH,
        )

    def fold_from(k):
        return pltpu.make_async_remote_copy(
            src_ref=got_z.at[k], dst_ref=got_z.at[k], send_sem=rz_send.at[k], recv_sem=rz_recv.at[k],
            device_id={"dp": k}, device_id_type=MESH,
        )

    for step in range(1, planes):
        fold(lax.rem(z + step, planes)).start()
    got_z[z] = tiles[z]
    for step in range(1, planes):
        fold_from(lax.rem(z + step, planes)).wait_recv()
    total = got_z[0]
    for b in range(1, planes):
        total = total + got_z[b]
    got_p[j] = total

    def share(to):
        return pltpu.make_async_remote_copy(
            src_ref=got_p.at[j], dst_ref=got_p.at[j], send_sem=rp_send.at[to], recv_sem=rp_recv.at[j],
            device_id={"tensor": to}, device_id_type=MESH,
        )

    def share_from(k):
        return pltpu.make_async_remote_copy(
            src_ref=got_p.at[k], dst_ref=got_p.at[k], send_sem=rp_send.at[k], recv_sem=rp_recv.at[k],
            device_id={"tensor": k}, device_id_type=MESH,
        )

    for step in range(1, members):
        share(lax.rem(j + step, members)).start()
    for step in range(1, members):
        share_from(lax.rem(j + step, members)).wait_recv()
    total = got_p[0]
    for k in range(1, members):
        total = total + got_p[k]
    res_ref[...] = total

    og.drain()
    more.drain()
    act.drain()
    acts.drain()
    for level in range(planes):
        for n in range(chunks):
            @pl.when((z - level >= 0) & (z < planes - 1))
            def _():
                up(z - level, n).wait_send()

            @pl.when((z + level < planes) & (z > 0))
            def _():
                down(z + level, n).wait_send()
    for step in range(1, members):
        to = lax.rem(j + step, members)
        spread(to).wait_send()
        share(to).wait_send()
    for step in range(1, planes):
        to = lax.rem(z + step, planes)
        for g in range(group):
            lift(to, g).wait_send()
        fold(to).wait_send()


def fits(planes, members, activations, out_grads_t, in_basis, query_proj, seq_count):
    rows, feats = activations.shape
    width, tokens = out_grads_t.shape
    cols, span = in_basis.shape[1], query_proj.shape[2]
    return (
        members == 8 and planes % 2 == 0 and rows == tokens and rows % (16 * members) == 0
        and feats % 128 == 0 and cols % 128 == 0 and span % cols == 0 and width % 16 == 0
        and tokens % CHUNK == 0 and tokens > CHUNK and width > 32 and CHUNK % (rows // seq_count) == 0 and (rows // seq_count) % 128 == 0
        and seq_count <= 128 and query_proj.shape[0] <= 8
    )


def local(planes, members, activations, out_grads_t, in_basis, out_basis_t, query_proj, eigvals, damping, lengths):
    seq_count = lengths.shape[0]
    if not fits(planes, members, activations, out_grads_t, in_basis, query_proj, seq_count):
        return generic(activations, out_grads_t, in_basis, out_basis_t, query_proj, eigvals, damping, lengths)
    bf16, f32 = jnp.bfloat16, jnp.float32
    rows, feats = activations.shape
    width, tokens = out_grads_t.shape
    features, cols = in_basis.shape
    depth = out_basis_t.shape[1]
    queries, _, span = query_proj.shape
    seq_len = rows // seq_count
    part, chunks, group = rows // members, tokens // CHUNK, span // cols
    position = lax.broadcasted_iota(jnp.int32, (seq_count, seq_len), 1)
    keep = jnp.broadcast_to((position < lengths[:, None]).astype(f32).reshape(1, tokens), (8, tokens))
    any_space = pl.BlockSpec(memory_space=pl.ANY)
    vmem = pl.BlockSpec(memory_space=pltpu.VMEM)
    dma = pltpu.SemaphoreType.DMA
    res = pl.pallas_call(
        functools.partial(kernel, planes, seq_len),
        out_shape=jax.ShapeDtypeStruct((8, 128), f32),
        in_specs=[any_space] * 6 + [vmem, pl.BlockSpec(memory_space=pltpu.SMEM)],
        out_specs=vmem,
        scratch_shapes=[
            pltpu.VMEM((members * width, tokens), bf16),
            pltpu.VMEM((members, rows, feats), bf16),
            pltpu.VMEM((features, cols), bf16),
            pltpu.VMEM((width, depth), bf16),
            pltpu.VMEM((queries, width, span), bf16),
            pltpu.VMEM((width, span), f32),
            pltpu.VMEM((planes, rows, span), bf16),
            pltpu.VMEM((members, part, cols), bf16),
            pltpu.VMEM((rows, cols), bf16),
            pltpu.VMEM((rows, cols), f32),
            pltpu.VMEM((planes, chunks, width, CHUNK), bf16),
            pltpu.VMEM((width, CHUNK), f32),
            pltpu.VMEM((planes, chunks, 8, CHUNK), f32),
            pltpu.VMEM((planes, 8, 128), f32),
            pltpu.VMEM((planes, 8, 128), f32),
            pltpu.VMEM((members, 8, 128), f32),
            dma((6,)), dma((4, 11)), dma((4, 11)),
            dma((planes, chunks)), dma((planes, chunks)), dma((planes, chunks)), dma((planes, chunks)),
            dma((members,)), dma((members,)), dma((planes, group)), dma((planes, group)),
            dma((planes,)), dma((planes,)), dma((members,)), dma((members,)),
        ],
        compiler_params=pltpu.CompilerParams(
            collective_id=0, has_side_effects=True, vmem_limit_bytes=63 * 1024 * 1024
        ),
    )(activations, out_grads_t, in_basis, out_basis_t, query_proj, eigvals, keep, damping)
    norm_factor = (features * depth * seq_len) ** (-0.5)
    return res[:queries, :seq_count].T * norm_factor


def solution(mesh):
    placed = (
        P("dp", "tensor"),
        P("tensor", "dp"),
        P(None, "tensor"),
        P("tensor", None),
        P(None, "tensor", "dp"),
        P("tensor", "dp"),
        P(),
        P("dp"),
    )
    return jax.shard_map(
        functools.partial(local, mesh.shape["dp"], mesh.shape["tensor"]), mesh=mesh, in_specs=placed, out_specs=P("dp", None), check_vma=False
    )
```

```python
import functools

import jax
import jax.numpy as jnp
from jax import lax
from jax.experimental import pallas as pl
from jax.experimental.pallas import tpu as pltpu
from jax.sharding import PartitionSpec as P


def generic(activations, out_grads_t, in_basis, out_basis_t, query_proj, eigvals, damping, lengths):
    bf16, f32 = jnp.bfloat16, jnp.float32
    seq_count = lengths.shape[0]
    full_act = lax.all_gather(activations, "tensor", axis=1, tiled=True)
    token_rows = full_act.shape[0]
    seq_len = token_rows // seq_count
    act_local = jnp.dot(full_act, in_basis, preferred_element_type=f32).astype(bf16)
    act_full = lax.all_gather(act_local, "tensor", axis=1, tiled=True)
    features = act_full.shape[1]
    act_proj = lax.all_to_all(act_full, "dp", split_axis=1, concat_axis=0, tiled=True)
    grad_full = jnp.dot(
        out_basis_t, lax.all_gather(out_grads_t, "tensor", axis=0, tiled=True), preferred_element_type=f32
    )
    position = lax.broadcasted_iota(jnp.int32, (seq_count, seq_len), 1)
    keep = (position < lengths[:, None]).astype(f32).reshape(1, token_rows)
    grad_local = (grad_full * keep).astype(bf16)
    grad_proj = lax.all_gather(grad_local, "dp", axis=1, tiled=True)
    scaled = (query_proj.astype(f32) / (eigvals + damping[0])).astype(bf16)
    mixed = jnp.einsum("td,qjd->qjt", act_proj, scaled, preferred_element_type=f32)
    weighted = mixed * grad_proj.astype(f32)[None, :, :]
    query_count, width, tokens = weighted.shape
    partial_value = jnp.sum(weighted.reshape(query_count, width, tokens // seq_len, seq_len), axis=(1, 3)).T
    totals = lax.psum(partial_value, ("dp", "tensor"))
    mine = lax.dynamic_slice_in_dim(totals, lax.axis_index("dp") * seq_count, seq_count, 0)
    norm_factor = (features * out_basis_t.shape[1] * seq_len) ** (-0.5)
    return mine * norm_factor


MESH = pl.DeviceIdType.MESH
CHUNK = 256


def kernel(
    planes, seq_len, act_ref, og_ref, in_ref, out_ref, query_ref, eig_ref, keep_ref, damp_ref, res_ref,
    og_all, act_all, in_b, out_b, scaled, eig, a_all, a_part, a_loc, a_acc, g_all, g_acc, csum, tiles, got_z, got_p,
    load_sem, gs_send, gs_recv, up_send, up_recv, dn_send, dn_recv, xp_send, xp_recv, xz_send, xz_recv,
    rz_send, rz_recv, rp_send, rp_recv,
):
    bf16, f32 = jnp.bfloat16, jnp.float32
    z, j = lax.axis_index("dp"), lax.axis_index("tensor")
    members = act_all.shape[0]
    rows, feats = act_ref.shape
    width, tokens = og_ref.shape
    depth = out_b.shape[1]
    queries, span = scaled.shape[0], scaled.shape[2]
    part = rows // members
    chunks = tokens // CHUNK
    jx = j + 2 - 4 * lax.rem(j // 2, 2)
    jy = j + 4 - 8 * (j // 4)
    jd = jx + 4 - 8 * (j // 4)

    def mate(k):
        return k + 1 - 2 * lax.rem(k, 2)

    jp = mate(j)

    loads = [
        pltpu.make_async_copy(og_ref, og_all.at[pl.ds(pl.multiple_of(j * width, 16), width), :], load_sem.at[0]),
        pltpu.make_async_copy(act_ref, act_all.at[j], load_sem.at[1]),
        pltpu.make_async_copy(query_ref, scaled, load_sem.at[2]),
        pltpu.make_async_copy(eig_ref, eig, load_sem.at[3]),
        pltpu.make_async_copy(out_ref, out_b, load_sem.at[4]),
        pltpu.make_async_copy(in_ref, in_b, load_sem.at[5]),
    ]
    for load in loads:
        load.start()

    barrier = pltpu.get_barrier_semaphore()
    for step in range(1, members):
        pl.semaphore_signal(barrier, inc=1, device_id={"tensor": lax.rem(j + step, members)}, device_id_type=MESH)
    for step in range(1, planes):
        pl.semaphore_signal(barrier, inc=1, device_id={"dp": lax.rem(z + step, planes)}, device_id_type=MESH)
    pl.semaphore_wait(barrier, members + planes - 2)

    cut = (width // 2 + 15) // 16 * 16

    def og_rows(h):
        return (0, width) if h is None else ((0, cut), (cut, width - cut))[h]

    def og_view(lanes):
        def view(k, h):
            first, size = og_rows(h)
            return og_all.at[pl.ds(pl.multiple_of(k * width + first, 16), size), lanes]

        return view

    def og_own(lanes):
        return lambda h: og_ref.at[pl.ds(*og_rows(h)), lanes]

    def act_view(k, h):
        if h is None:
            return act_all.at[k]
        return act_all.at[k, pl.ds(h * (rows // 2), rows // 2), :]

    half = planes // 2
    side = z // half

    def a_view(turn):
        base = lax.rem(side + turn, 2) * half

        def view(k, h):
            at = pl.ds(pl.multiple_of(k * part, 16), part)
            if h is None:
                return a_all.at[pl.ds(base, half), at, :]
            return a_all.at[pl.ds(base + h * (half // 2), half // 2), at, :]

        return view

    def a_own(turn):
        return lambda h: a_view(turn)(j, h)

    class Gather:
        def __init__(self, op, view, own):
            self.op, self.view, self.own = op, view, own
            self.plan = [
                (j, 0, jx), (j, 1, jx), (jy, 1, jx),
                (j, 1, jy), (j, 0, jy), (jx, 0, jy),
                (j, None, jp), (jx, None, jp), (jy, None, jp), (jd, 0, jp), (jd, 1, jp),
            ]
            self.landed = [
                (jx, 0), (jx, 1), (jd, 1),
                (jy, 1), (jy, 0), (jd, 0),
                (jp, None), (mate(jx), None), (mate(jy), None), (mate(jd), 0), (mate(jd), 1),
            ]

        def copy(self, slot):
            block, half, target = self.plan[slot]
            src = self.own(half) if slot in (0, 1, 3, 4, 6) else self.view(block, half)
            return pltpu.make_async_remote_copy(
                src_ref=src, dst_ref=self.view(block, half), send_sem=gs_send.at[self.op, slot],
                recv_sem=gs_recv.at[self.op, slot], device_id={"tensor": target}, device_id_type=MESH,
            )

        def start(self, *slots):
            for slot in slots:
                self.copy(slot).start()

        def arrive(self, *slots):
            for slot in slots:
                block, half = self.landed[slot]
                view = self.view(block, half)
                pltpu.make_async_remote_copy(
                    src_ref=view, dst_ref=view, send_sem=gs_send.at[self.op, slot],
                    recv_sem=gs_recv.at[self.op, slot], device_id={"tensor": jp}, device_id_type=MESH,
                ).wait_recv()

        def open(self):
            self.start(0, 3, 6)

        def extend(self):
            self.start(1, 4)

        def begin(self):
            self.start(0, 3, 1, 4, 6)

        def relay(self):
            self.arrive(0)
            self.start(5)
            self.arrive(3)
            self.start(2)

        def share_near(self):
            self.arrive(1)
            self.start(7)
            self.arrive(4)
            self.start(8)

        def share_far(self):
            self.arrive(5)
            self.start(9)
            self.arrive(2)
            self.start(10)

        def drain(self):
            for slot in range(len(self.plan)):
                self.copy(slot).wait_send()

    def act_own(h):
        return act_ref if h is None else act_ref.at[pl.ds(h * (rows // 2), rows // 2), :]

    lanes = [pl.ds(0, CHUNK), pl.ds(CHUNK, CHUNK), pl.ds(2 * CHUNK, tokens - 2 * CHUNK)]
    og, next_og, more = [Gather(op, og_view(at), og_own(at)) for op, at in zip((0, 4, 3), lanes)]
    act = Gather(1, act_view, act_own)
    near, far = [Gather(op, a_view(turn), a_own(turn)) for op, turn in ((2, 0), (5, 1))]

    og.begin()
    csum[...] = jnp.zeros_like(csum)

    loads[2].wait()
    loads[3].wait()
    step_rows = 16

    def scale(i, carry):
        at = pl.ds(pl.multiple_of(i * step_rows, step_rows), step_rows)
        below = eig[at, :] + damp_ref[0]
        for q in range(queries):
            scaled[q, at, :] = (scaled[q, at, :].astype(f32) / below).astype(bf16)
        return carry

    lax.fori_loop(0, width // step_rows, scale, 0)

    og.relay()
    next_og.begin()
    og.share_near()
    og.share_far()
    og.arrive(6, 7, 8, 9, 10)
    loads[0].wait()
    loads[4].wait()

    def up(block, n):
        return pltpu.make_async_remote_copy(
            src_ref=g_all.at[block, n], dst_ref=g_all.at[block, n], send_sem=up_send.at[block, n],
            recv_sem=up_recv.at[block, n], device_id={"dp": lax.rem(z + 1, planes)}, device_id_type=MESH,
        )

    def down(block, n):
        return pltpu.make_async_remote_copy(
            src_ref=g_all.at[block, n], dst_ref=g_all.at[block, n], send_sem=dn_send.at[block, n],
            recv_sem=dn_recv.at[block, n], device_id={"dp": lax.rem(z + planes - 1, planes)}, device_id_type=MESH,
        )

    top, bottom = z == planes - 1, z == 0

    def service(level, n):
        @pl.when(z - level >= 0)
        def _():
            up(z - level, n).wait_recv()

        @pl.when((z - level >= 0) & (z < planes - 1))
        def _():
            up(z - level, n).start()

        @pl.when(z + level < planes)
        def _():
            down(z + level, n).wait_recv()

        @pl.when((z + level < planes) & (z > 0))
        def _():
            down(z + level, n).start()

    k_tile = 3 * CHUNK
    k_full = depth // k_tile

    def project(n, carry):
        at = pl.ds(pl.multiple_of(n * CHUNK, CHUNK), CHUNK)
        k_rest = depth - k_full * k_tile
        if k_rest:
            g_acc[...] = jnp.dot(
                out_b[:, pl.ds(k_full * k_tile, k_rest)], og_all[pl.ds(k_full * k_tile, k_rest), at],
                preferred_element_type=f32,
            )
        else:
            g_acc[...] = jnp.zeros_like(g_acc)

        def inner(k, c):
            deep = pl.ds(pl.multiple_of(k * k_tile, k_tile), k_tile)
            g_acc[...] += jnp.dot(out_b[:, deep], og_all[deep, at], preferred_element_type=f32)
            return c

        lax.fori_loop(0, k_full, inner, 0)
        g_all[z, n] = (g_acc[...] * keep_ref[0:1, at]).astype(bf16)

        @pl.when(z < planes - 1)
        def _():
            up(z, n).start()

        @pl.when(z > 0)
        def _():
            down(z, n).start()

        return carry

    project(0, 0)
    next_og.relay()
    act.begin()
    next_og.share_near()
    next_og.share_far()
    next_og.arrive(6, 7, 8, 9, 10)
    lax.fori_loop(1, 2, project, 0)
    service(1, 0)

    a_acc[...] = jnp.zeros_like(a_acc)
    loads[1].wait()
    loads[5].wait()

    def contract(first):
        def body(i, carry):
            k = first + i * (mate(first) - first)
            deep = pl.ds(pl.multiple_of(k * feats, feats), feats)
            a_acc[...] += jnp.dot(act_all[k], in_b[deep, :], preferred_element_type=f32)
            return carry

        lax.fori_loop(0, 2, body, 0)

    act.relay()
    more.open()
    act.arrive(6)
    contract(j)
    service(2, 0)
    act.share_near()
    act.arrive(7)
    contract(jx)
    act.arrive(8)
    contract(jy)
    service(1, 1)
    act.share_far()
    act.arrive(9, 10)
    contract(jd)
    a_loc[...] = a_acc[...].astype(bf16)

    def spread(to):
        return pltpu.make_async_remote_copy(
            src_ref=a_loc.at[pl.ds(pl.multiple_of(to * part, 16), part), :],
            dst_ref=a_part.at[j], send_sem=xp_send.at[to], recv_sem=xp_recv.at[j],
            device_id={"tensor": to}, device_id_type=MESH,
        )

    def spread_from(k):
        return pltpu.make_async_remote_copy(
            src_ref=a_part.at[k], dst_ref=a_part.at[k], send_sem=xp_send.at[k], recv_sem=xp_recv.at[k],
            device_id={"tensor": k}, device_id_type=MESH,
        )

    for step in range(1, members):
        spread(lax.rem(j + step, members)).start()
    a_part[j] = a_loc[pl.ds(pl.multiple_of(j * part, 16), part), :]
    more.extend()
    service(3, 0)
    service(2, 1)
    more.relay()
    for step in range(1, members):
        spread_from(lax.rem(j + step, members)).wait_recv()

    mine = pl.ds(pl.multiple_of(j * part, 16), part)
    group = span // a_part.shape[2]

    def lift(to, g):
        lane = pl.ds(g * a_part.shape[2], a_part.shape[2])
        return pltpu.make_async_remote_copy(
            src_ref=a_part.at[to * group + g], dst_ref=a_all.at[z, mine, lane], send_sem=xz_send.at[to, g],
            recv_sem=xz_recv.at[z, g], device_id={"dp": to}, device_id_type=MESH,
        )

    def lift_from(k, g):
        lane = pl.ds(g * a_part.shape[2], a_part.shape[2])
        view = a_all.at[k, mine, lane]
        return pltpu.make_async_remote_copy(
            src_ref=view, dst_ref=view, send_sem=xz_send.at[k, g], recv_sem=xz_recv.at[k, g],
            device_id={"dp": k}, device_id_type=MESH,
        )

    for step in range(1, planes):
        for g in range(group):
            lift(lax.rem(z + step, planes), g).start()
    for g in range(group):
        a_all[z, mine, pl.ds(g * a_part.shape[2], a_part.shape[2])] = a_part[z * group + g]
    more.share_near()
    service(3, 1)
    more.share_far()
    for step in range(1, planes):
        for g in range(group):
            lift_from(lax.rem(z + step, planes), g).wait_recv()
    near.begin()
    more.arrive(6, 7, 8, 9, 10)
    lax.fori_loop(2, chunks, project, 0)
    near.relay()
    far.begin()
    near.share_near()
    for n in range(2, chunks):
        service(1, n)
    near.share_far()
    near.arrive(6, 7, 8, 9, 10)
    for level in range(4, planes):
        for n in range(2):
            service(level, n)

    def score(s, n):
        ahead = side * half + lax.rem(z - side * half + s, half)
        other = s - half
        across = (1 - side) * half + (1 - side) * other + side * (half - 1 - other)
        block = ahead + (s // half) * (across - ahead)
        at = pl.ds(pl.multiple_of(n * CHUNK, CHUNK), CHUNK)
        for q in range(queries):
            mixed = lax.dot_general(
                scaled[q], a_all[block, at, :], (((1,), (1,)), ((), ())), preferred_element_type=f32
            )
            csum[block, n, pl.ds(q, 1), :] = jnp.sum(mixed * g_all[block, n].astype(f32), axis=0, keepdims=True)

    def score_loop(lo, hi, n):
        def body(s, carry):
            score(s, n)
            return carry

        lax.fori_loop(lo, hi, body, 0)

    score_loop(0, half, 0)
    far.relay()
    score_loop(0, half, 1)
    far.share_near()
    for n in range(2, chunks):
        service(2, n)
    far.share_far()
    for n in range(2, chunks):
        score_loop(0, half, n)
    far.arrive(6, 7, 8, 9, 10)
    score_loop(half, planes, 0)
    score_loop(half, planes, 1)
    for level in range(3, planes):
        for n in range(2, chunks):
            service(level, n)
    for n in range(2, chunks):
        score_loop(half, planes, n)

    per = res_ref.shape[1]
    lane_at = lax.broadcasted_iota(jnp.int32, (8, per), 1)
    each = CHUNK // seq_len
    for b in range(planes):
        tile = jnp.zeros((8, per), f32)
        for n in range(chunks):
            for h in range(each):
                total = jnp.sum(csum[b, n, :, h * seq_len:(h + 1) * seq_len], axis=1, keepdims=True)
                tile = tile + jnp.where(lane_at == n * each + h, total, 0.0)
        tiles[b] = tile

    def fold(to):
        return pltpu.make_async_remote_copy(
            src_ref=tiles.at[to], dst_ref=got_z.at[z], send_sem=rz_send.at[to], recv_sem=rz_recv.at[z],
            device_id={"dp": to}, device_id_type=MESH,
        )

    def fold_from(k):
        return pltpu.make_async_remote_copy(
            src_ref=got_z.at[k], dst_ref=got_z.at[k], send_sem=rz_send.at[k], recv_sem=rz_recv.at[k],
            device_id={"dp": k}, device_id_type=MESH,
        )

    for step in range(1, planes):
        fold(lax.rem(z + step, planes)).start()
    got_z[z] = tiles[z]
    for step in range(1, planes):
        fold_from(lax.rem(z + step, planes)).wait_recv()
    total = got_z[0]
    for b in range(1, planes):
        total = total + got_z[b]
    got_p[j] = total

    def share(to):
        return pltpu.make_async_remote_copy(
            src_ref=got_p.at[j], dst_ref=got_p.at[j], send_sem=rp_send.at[to], recv_sem=rp_recv.at[j],
            device_id={"tensor": to}, device_id_type=MESH,
        )

    def share_from(k):
        return pltpu.make_async_remote_copy(
            src_ref=got_p.at[k], dst_ref=got_p.at[k], send_sem=rp_send.at[k], recv_sem=rp_recv.at[k],
            device_id={"tensor": k}, device_id_type=MESH,
        )

    for step in range(1, members):
        share(lax.rem(j + step, members)).start()
    for step in range(1, members):
        share_from(lax.rem(j + step, members)).wait_recv()
    total = got_p[0]
    for k in range(1, members):
        total = total + got_p[k]
    res_ref[...] = total

    og.drain()
    next_og.drain()
    more.drain()
    act.drain()
    near.drain()
    far.drain()
    for level in range(planes):
        for n in range(chunks):
            @pl.when((z - level >= 0) & (z < planes - 1))
            def _():
                up(z - level, n).wait_send()

            @pl.when((z + level < planes) & (z > 0))
            def _():
                down(z + level, n).wait_send()
    for step in range(1, members):
        to = lax.rem(j + step, members)
        spread(to).wait_send()
        share(to).wait_send()
    for step in range(1, planes):
        to = lax.rem(z + step, planes)
        for g in range(group):
            lift(to, g).wait_send()
        fold(to).wait_send()


def fits(planes, members, activations, out_grads_t, in_basis, query_proj, seq_count):
    rows, feats = activations.shape
    width, tokens = out_grads_t.shape
    cols, span = in_basis.shape[1], query_proj.shape[2]
    return (
        members == 8 and planes == 4 and rows == tokens and rows % (16 * members) == 0
        and feats % 128 == 0 and cols % 128 == 0 and span % cols == 0 and width % 16 == 0
        and tokens % CHUNK == 0 and tokens > 2 * CHUNK and width > 32 and CHUNK % (rows // seq_count) == 0 and (rows // seq_count) % 128 == 0
        and seq_count <= 128 and query_proj.shape[0] <= 8
    )


def local(planes, members, activations, out_grads_t, in_basis, out_basis_t, query_proj, eigvals, damping, lengths):
    seq_count = lengths.shape[0]
    if not fits(planes, members, activations, out_grads_t, in_basis, query_proj, seq_count):
        return generic(activations, out_grads_t, in_basis, out_basis_t, query_proj, eigvals, damping, lengths)
    bf16, f32 = jnp.bfloat16, jnp.float32
    rows, feats = activations.shape
    width, tokens = out_grads_t.shape
    features, cols = in_basis.shape
    depth = out_basis_t.shape[1]
    queries, _, span = query_proj.shape
    seq_len = rows // seq_count
    part, chunks, group = rows // members, tokens // CHUNK, span // cols
    position = lax.broadcasted_iota(jnp.int32, (seq_count, seq_len), 1)
    keep = jnp.broadcast_to((position < lengths[:, None]).astype(f32).reshape(1, tokens), (8, tokens))
    any_space = pl.BlockSpec(memory_space=pl.ANY)
    vmem = pl.BlockSpec(memory_space=pltpu.VMEM)
    dma = pltpu.SemaphoreType.DMA
    res = pl.pallas_call(
        functools.partial(kernel, planes, seq_len),
        out_shape=jax.ShapeDtypeStruct((8, 128), f32),
        in_specs=[any_space] * 6 + [vmem, pl.BlockSpec(memory_space=pltpu.SMEM)],
        out_specs=vmem,
        scratch_shapes=[
            pltpu.VMEM((members * width, tokens), bf16),
            pltpu.VMEM((members, rows, feats), bf16),
            pltpu.VMEM((features, cols), bf16),
            pltpu.VMEM((width, depth), bf16),
            pltpu.VMEM((queries, width, span), bf16),
            pltpu.VMEM((width, span), f32),
            pltpu.VMEM((planes, rows, span), bf16),
            pltpu.VMEM((members, part, cols), bf16),
            pltpu.VMEM((rows, cols), bf16),
            pltpu.VMEM((rows, cols), f32),
            pltpu.VMEM((planes, chunks, width, CHUNK), bf16),
            pltpu.VMEM((width, CHUNK), f32),
            pltpu.VMEM((planes, chunks, 8, CHUNK), f32),
            pltpu.VMEM((planes, 8, 128), f32),
            pltpu.VMEM((planes, 8, 128), f32),
            pltpu.VMEM((members, 8, 128), f32),
            dma((6,)), dma((6, 11)), dma((6, 11)),
            dma((planes, chunks)), dma((planes, chunks)), dma((planes, chunks)), dma((planes, chunks)),
            dma((members,)), dma((members,)), dma((planes, group)), dma((planes, group)),
            dma((planes,)), dma((planes,)), dma((members,)), dma((members,)),
        ],
        compiler_params=pltpu.CompilerParams(
            collective_id=0, has_side_effects=True, vmem_limit_bytes=63 * 1024 * 1024
        ),
    )(activations, out_grads_t, in_basis, out_basis_t, query_proj, eigvals, keep, damping)
    norm_factor = (features * depth * seq_len) ** (-0.5)
    return res[:queries, :seq_count].T * norm_factor


def solution(mesh):
    placed = (
        P("dp", "tensor"),
        P("tensor", "dp"),
        P(None, "tensor"),
        P("tensor", None),
        P(None, "tensor", "dp"),
        P("tensor", "dp"),
        P(),
        P("dp"),
    )
    return jax.shard_map(
        functools.partial(local, mesh.shape["dp"], mesh.shape["tensor"]), mesh=mesh, in_specs=placed, out_specs=P("dp", None), check_vma=False
    )
```
